256 devices in a mesh: expert: 8 (over x_hi, y), dp: 32 (over x_lo, z, core).
Axes of the slice: x: 4 (x_hi: 2, x_lo: 2; x = x_hi * 2 + x_lo), y: 4, z: 8, core: 2. Of those that a mesh axis runs over, the one named last changes fastest.
Arguments:
- tokens: bfloat16 [2048, 4096], P(('expert', 'dp')), may hold values from -6 to 6
- routes: int32 [2048, 2], P(('expert', 'dp')), may hold values from 0 to 7, all different within a row; in each aligned block of 8 rows (0 to 7, 8 to 15, ...) at most 3 rows name the same one
- route_weights: float32 [2048, 2], P(('expert', 'dp')), may hold values from 0.2 to 1
- w_gate: bfloat16 [8, 4096, 14336], P('expert', None, 'dp'), may hold values from -0.09375 to 0.09375
- w_up: bfloat16 [8, 4096, 14336], P('expert', None, 'dp'), may hold values from -0.09375 to 0.09375
- w_down: bfloat16 [8, 14336, 4096], P('expert', 'dp'), may hold values from -0.046875 to 0.046875
Outputs:
- mixed: bfloat16 [2048, 4096], P(('expert', 'dp'))
The draws below stay inside these ranges and needn't reach their ends.
Inputs may be any that keep to these rules, and one draw needn't show every extreme that they name: `routes`: within the rows of one device (aligned blocks of 8 rows) the two experts of a token differ and no expert is named more than 3 times; in every draw some block names some expert exactly 3 times. Every expert is named somewhere.
All inputs are finite; a program needn't handle non-finite values.
Results may differ from the reference program's by a relative error of at most 0.0057.
Values may be sent and summed in bfloat16 or wider, within the bound.
No kernel may reach another device: no remote copies, remote signals or barrier semaphores. Data moves between devices by JAX's collectives and lax.ppermute only.
A program may use at most 128 MiB of HBM per device.

```python
import math
import jax
import jax.numpy as jnp
import numpy as np
from jax import lax

D = 4096
FF = 14336
TOK_DEV = 8
EXPERTS = 8
CAP = 3
TOKENS = 2048
N_EXPERT = 8
N_DP = 32


def levels(own_key, extent, cuts, low, top_value):
    loudness, own = 1.0, jax.random.fold_in(own_key, 6)
    for axis_at, blocks in cuts:
        steps = jnp.exp(jax.random.uniform(jax.random.fold_in(own, axis_at), (blocks,), jnp.float32, low / len(cuts), top_value / len(cuts)))
        loudness = loudness * jnp.repeat(steps, extent[axis_at] // blocks).reshape([-1 if axis == axis_at else 1 for axis in range(len(extent))])
    return loudness


def routed_block(key, own, number, rows, count, top, limit, skew):
    order = jax.random.permutation(key, count)
    heavy_load, common = shares(count, rows * top, limit, skew, True), shares(count, rows * top, limit, skew, False)
    places = jnp.arange(count)

    def named(lengths, rotation):
        used = int((lengths > 0).sum())
        fixed = max(1, used // 4)
        moved = fixed + (places - fixed + rotation * (used - fixed)) % max(1, count - fixed)
        return jnp.zeros((count,), jnp.int32).at[order[jnp.where(places < fixed, places, moved)]].set(jnp.asarray(lengths, jnp.int32))

    lengths = jnp.where(number % 4 == 0, named(heavy_load, number // 4), named(common, number - number // 4 - 1))
    mixed = jax.random.permutation(jax.random.fold_in(own, 3), count)
    giver, sink = mixed[0:count // 2 * 2:2], mixed[1:count // 2 * 2:2]
    room = jnp.minimum(lengths[giver] - 1, limit - lengths[sink]) // 2
    room = jnp.where((giver == order[0]) | (sink == order[0]) | (lengths[sink] == 0), 0, jnp.maximum(room, 0))
    moved = jax.random.randint(jax.random.fold_in(own, 4), (count // 2,), 0, 1 << 20) % (room + 1)
    lengths = lengths.at[giver].add(-moved).at[sink].add(moved)
    items = jnp.searchsorted(jnp.cumsum(lengths), jnp.arange(rows * top), side="right").astype(jnp.int32)
    table = items.reshape(top, rows).T
    table = table[jax.random.permutation(jax.random.fold_in(own, 1), rows)]
    rotation = jax.random.randint(jax.random.fold_in(own, 2), (rows, 1), 0, top)
    return jnp.take_along_axis(table, (jnp.arange(top)[None, :] + rotation) % top, axis=1)


def shares(amount, total, reach, slope, full):
    weights = [(1 << 20) // math.isqrt(rank ** slope) + 1 for rank in range(1, amount + 1)]
    largest = reach if full else min(reach, max(-(-total // amount), total * weights[0] // sum(weights)))
    least = 1 if total - largest >= amount - 1 else 0
    counts, rest = [largest] + [least] * (amount - 1), total - largest - least * (amount - 1)
    while rest > 0:
        candidates = [i for i in range(1, amount) if counts[i] < largest] or [i for i in range(1, amount) if counts[i] < reach]
        whole, remaining = sum([weights[i] for i in candidates]), rest
        for i in candidates:
            addition = min(reach - counts[i], max(1, remaining * weights[i] // whole), rest)
            counts[i] = counts[i] + addition
            rest = rest - addition
    return np.array(counts)


def centred(own_key, shape, spread, most, cuts=(), kind=jnp.bfloat16):
    factor_of = levels(own_key, shape, cuts, -0.22, 0.18) if cuts else 1.0
    values = jax.random.normal(own_key, shape, jnp.float32) * spread * factor_of
    return jnp.minimum(jnp.maximum(values, -most), most).astype(kind)


def setup_inputs(seed: int = 0) -> dict:
    keys = jax.random.split(jax.random.key(seed), 7)
    tokens = centred(keys[0], (TOKENS, D), 1.0, 6.0, ((0, 256),))
    routes_keys = jax.random.split(jax.random.fold_in(keys[1], 1), TOKENS // TOK_DEV)
    routes_turns = jax.random.permutation(jax.random.fold_in(keys[1], 3), TOKENS // TOK_DEV)
    routes = jax.vmap(lambda own, number: routed_block(jax.random.fold_in(keys[1], 2), own, number, TOK_DEV, EXPERTS, 2, CAP, 2))(routes_keys, routes_turns).reshape((TOKENS, 2))
    route_weights = jnp.clip(0.2 + 0.8 * jax.random.uniform(keys[2], (TOKENS, 2), jnp.float32) ** levels(keys[2], (TOKENS, 2), ((0, 256),), -0.2, 0.2), 0.2, 1.0)
    w_gate = centred(keys[3], (EXPERTS, D, FF), D ** -0.5, 0.09375, ((0, 8), (2, 32)))
    w_up = centred(keys[4], (EXPERTS, D, FF), D ** -0.5, 0.09375, ((0, 8), (2, 32)))
    w_down = centred(keys[5], (EXPERTS, FF, D), FF ** -0.5, 0.046875, ((0, 8), (1, 32)))
    return dict(tokens=tokens, routes=routes, route_weights=route_weights, w_gate=w_gate, w_up=w_up, w_down=w_down)


def slot_columns(routes):
    devices = N_EXPERT * N_DP
    listed = routes.reshape(devices, TOK_DEV * 2)
    chosen = (listed[:, :, None] == jnp.arange(EXPERTS, dtype=jnp.int32)[None, None, :]).astype(jnp.int32)
    before = jnp.cumsum(chosen, axis=1) - chosen
    return listed * CAP + jnp.sum(before * chosen, axis=2)


def reference(tokens, routes, route_weights, w_gate, w_up, w_down):
    devices = N_EXPERT * N_DP
    columns = EXPERTS * CAP
    slice_units = FF // N_DP
    column = slot_columns(routes)
    placing = (column[:, :, None] == jnp.arange(columns, dtype=jnp.int32)[None, None, :]).astype(jnp.float32)
    placing = placing.reshape(devices, TOK_DEV, 2, columns)
    sending = jnp.sum(placing, axis=2)
    token_blocks = tokens.reshape(devices, TOK_DEV, D).astype(jnp.float32)
    outgoing = jnp.einsum("ntw,ntd->nwd", sending, token_blocks).astype(jnp.bfloat16)
    expert_rows = outgoing.reshape(devices, EXPERTS, CAP, D).transpose(1, 0, 2, 3).reshape(EXPERTS, devices * CAP, D)

    def one_expert(operands):
        inputs, gate_full, up_full, down_full = operands
        gate_slices = gate_full.reshape(D, N_DP, slice_units).transpose(1, 0, 2)
        up_slices = up_full.reshape(D, N_DP, slice_units).transpose(1, 0, 2)
        down_slices = down_full.reshape(N_DP, slice_units, D)

        def add_slice(total, pieces):
            gate_piece, up_piece, down_piece = pieces
            gated = jnp.dot(inputs, gate_piece, preferred_element_type=jnp.float32)
            upward = jnp.dot(inputs, up_piece, preferred_element_type=jnp.float32)
            hidden = (jax.nn.silu(gated) * upward).astype(jnp.bfloat16)
            part = jnp.dot(hidden, down_piece, preferred_element_type=jnp.float32)
            return total + part, None

        start_total = jnp.zeros((inputs.shape[0], D), jnp.float32)
        total, unused = lax.scan(add_slice, start_total, (gate_slices, up_slices, down_slices))
        return total.astype(jnp.bfloat16)

    expert_out = lax.map(one_expert, (expert_rows, w_gate, w_up, w_down))
    returned = expert_out.reshape(EXPERTS, devices, CAP, D).transpose(1, 0, 2, 3).reshape(devices, columns, D)
    picked = jnp.einsum("ntkw,nwd->ntkd", placing, returned.astype(jnp.float32))
    weights = route_weights.reshape(devices, TOK_DEV, 2)
    mixed = jnp.sum(weights[:, :, :, None] * picked, axis=2)
    return mixed.reshape(TOKENS, D).astype(jnp.bfloat16)
```

```python
import jax
import jax.numpy as jnp
from jax import lax
from jax.sharding import Mesh
from jax.sharding import PartitionSpec as P
from jax.experimental import pallas as pl
from jax.experimental.pallas import tpu as pltpu

EXPERT = ("xh", "y")
LINE = ("xl", "z")
ALL = ("xh", "y", "xl", "z", "c")
PIECES = 3
CUTS = 4
SWAP = [(0, 1), (1, 0)]


def expert_kernel(
    own_ref, other_ref, gate_in, up_in, down_in, keep_ref, give_ref, gate, up, down, sems
):
    count, features = own_ref.shape
    depth = features // CUTS
    arriving = []
    for cut in range(CUTS):
        span = pl.ds(cut * depth, depth)
        arriving.append(
            (
                pltpu.make_async_copy(gate_in.at[:, span], gate.at[:, span], sems.at[cut]),
                pltpu.make_async_copy(up_in.at[:, span], up.at[:, span], sems.at[CUTS + cut]),
            )
        )
    last = pltpu.make_async_copy(down_in, down, sems.at[2 * CUTS])
    for pair in arriving:
        for copy in pair:
            copy.start()
    last.start()
    gated = jnp.zeros((2 * count, gate.shape[0]), jnp.float32)
    upward = jnp.zeros((2 * count, gate.shape[0]), jnp.float32)
    across = (((1,), (1,)), ((), ()))
    for cut in range(CUTS):
        span = pl.ds(cut * depth, depth)
        block = jnp.concatenate([own_ref[:, span], other_ref[:, span]], axis=0)
        for copy in arriving[cut]:
            copy.wait()
        gated += lax.dot_general(block, gate[:, span], across, preferred_element_type=jnp.float32)
        upward += lax.dot_general(block, up[:, span], across, preferred_element_type=jnp.float32)
    hidden = (gated / (1.0 + jnp.exp(-gated)) * upward).astype(jnp.bfloat16)
    last.wait()
    half = count // 2
    unit = count // 16
    for cut in range(CUTS):
        span = pl.ds(cut * depth, depth)
        part = jnp.dot(hidden, down[:, span], preferred_element_type=jnp.float32)
        for block in range(16):
            source = (block % 2) * half + (block // 2) * unit
            target = pl.ds(block * unit, unit)
            keep_ref[target, span] = part[source : source + unit]
            give_ref[target, span] = part[count + source : count + source + unit].astype(
                jnp.bfloat16
            )


def project(own, other, gate, up, down):
    count, features = own.shape
    units = gate.shape[0]
    whole = pl.BlockSpec(memory_space=pltpu.VMEM)
    outside = pl.BlockSpec(memory_space=pl.ANY)
    return pl.pallas_call(
        expert_kernel,
        out_shape=(
            jax.ShapeDtypeStruct((count, features), jnp.float32),
            jax.ShapeDtypeStruct((count, features), jnp.bfloat16),
        ),
        in_specs=[whole, whole, outside, outside, outside],
        out_specs=(whole, whole),
        scratch_shapes=[
            pltpu.VMEM((units, features), jnp.bfloat16),
            pltpu.VMEM((units, features), jnp.bfloat16),
            pltpu.VMEM((units, features), jnp.bfloat16),
            pltpu.SemaphoreType.DMA((2 * CUTS + 1,)),
        ],
        cost_estimate=pl.CostEstimate(
            flops=12 * count * features * units,
            bytes_accessed=6 * units * features + 10 * count * features,
            transcendentals=2 * count * units,
        ),
        compiler_params=pltpu.CompilerParams(vmem_limit_bytes=40 * 1024 * 1024),
        name="expert",
    )(own, other, gate, up, down)


def local(tokens, routes, route_weights, w_gate, w_up, w_down):
    groups = lax.axis_size("xh") * lax.axis_size("y")
    tok_count = tokens.shape[0]
    features = tokens.shape[1]
    capacity = 3 * tok_count // groups
    columns = groups * capacity
    listed = routes.reshape(2 * tok_count)
    chosen = (listed[:, None] == jnp.arange(groups, dtype=jnp.int32)[None, :]).astype(jnp.int32)
    before = jnp.cumsum(chosen, axis=0) - chosen
    column = listed * capacity + jnp.sum(before * chosen, axis=1)
    placing = (column[:, None] == jnp.arange(columns, dtype=jnp.int32)[None, :]).astype(
        jnp.bfloat16
    )
    placing = placing.reshape(tok_count, 2, columns)
    sending = jnp.sum(placing, axis=1)
    outgoing = jnp.einsum("tw,td->wd", sending, tokens, preferred_element_type=jnp.float32).astype(
        jnp.bfloat16
    )
    arrived = lax.all_to_all(
        outgoing.reshape(groups, capacity, features), EXPERT, split_axis=0, concat_axis=0, tiled=True
    )
    arrived = arrived.reshape(columns, features)
    step = columns // PIECES
    lined = [
        lax.all_gather(arrived[i * step : (i + 1) * step], LINE, axis=0, tiled=True)
        for i in range(PIECES)
    ]
    side = lax.axis_index("xl")
    gate = jnp.swapaxes(w_gate[0], 0, 1)
    up = jnp.swapaxes(w_up[0], 0, 1)
    finished = []
    give = None
    for own in lined:
        if give is not None:
            own, give = lax.optimization_barrier((own, give))
            pending.append((keep, lax.ppermute(give, "c", SWAP)))
        else:
            pending = []
        other = lax.ppermute(own, "c", SWAP)
        keep, give = project(own, other, gate, up, w_down[0])
    pending.append((keep, lax.ppermute(give, "c", SWAP)))
    for keep, swapped in pending:
        paired = (keep + swapped.astype(jnp.float32)).astype(jnp.bfloat16)
        along = lax.psum_scatter(paired, "z", scatter_dimension=0, tiled=True)
        mine = lax.dynamic_slice_in_dim(along, side * step, step)
        theirs = lax.dynamic_slice_in_dim(along, (1 - side) * step, step)
        crossed = lax.ppermute(theirs, "xl", SWAP)
        finished.append(
            (mine.astype(jnp.float32) + crossed.astype(jnp.float32)).astype(jnp.bfloat16)
        )
    results = jnp.concatenate(finished).reshape(groups, capacity, features)
    returned = lax.all_to_all(results, EXPERT, split_axis=0, concat_axis=0, tiled=True).reshape(
        columns, features
    )
    picked = jnp.einsum("tkw,wd->tkd", placing, returned, preferred_element_type=jnp.float32)
    combined = jnp.sum(route_weights[:, :, None] * picked, axis=1)
    return combined.astype(jnp.bfloat16)


def solution(mesh):
    fine = Mesh(mesh.devices.reshape(2, 4, 2, 8, 2), ALL)
    placed = (
        P(ALL, None),
        P(ALL, None),
        P(ALL, None),
        P(EXPERT, None, ("xl", "z", "c")),
        P(EXPERT, None, ("xl", "z", "c")),
        P(EXPERT, ("xl", "z", "c"), None),
    )
    return jax.shard_map(
        local, mesh=fine, in_specs=placed, out_specs=P(ALL, None), check_vma=False
    )
```

```python
import jax
import jax.numpy as jnp
from jax import lax
from jax.sharding import Mesh
from jax.sharding import PartitionSpec as P
from jax.experimental import pallas as pl
from jax.experimental.pallas import tpu as pltpu

EXPERT = ("xh", "y")
ALL = ("xh", "y", "xl", "z", "c")
RING = ("z", "c")
SWAP = [(0, 1), (1, 0)]
CUTS = 4


def load_kernel(gate_in, up_in, down_in, gate, up, down, sems):
    copies = [
        pltpu.make_async_copy(gate_in, gate, sems.at[0]),
        pltpu.make_async_copy(up_in, up, sems.at[1]),
        pltpu.make_async_copy(down_in, down, sems.at[2]),
    ]
    for copy in copies:
        copy.start()
    for copy in copies:
        copy.wait()


def load(gate, up, down):
    whole = pl.BlockSpec(memory_space=pltpu.VMEM)
    outside = pl.BlockSpec(memory_space=pl.ANY)
    return pl.pallas_call(
        load_kernel,
        out_shape=[jax.ShapeDtypeStruct(w.shape, w.dtype) for w in (gate, up, down)],
        in_specs=[outside] * 3,
        out_specs=[whole] * 3,
        scratch_shapes=[pltpu.SemaphoreType.DMA((3,))],
        name="load",
    )(gate, up, down)


def expert_kernel(own_ref, other_ref, gate_ref, up_ref, down_ref, keep_ref, give_ref):
    count, features = own_ref.shape
    across = (((1,), (1,)), ((), ()))
    block = jnp.concatenate([own_ref[...], other_ref[...]], axis=0)
    gated = lax.dot_general(block, gate_ref[...], across, preferred_element_type=jnp.float32)
    upward = lax.dot_general(block, up_ref[...], across, preferred_element_type=jnp.float32)
    hidden = (gated / (1.0 + jnp.exp(-gated)) * upward).astype(jnp.bfloat16)
    depth = features // CUTS
    for cut in range(CUTS):
        span = pl.ds(cut * depth, depth)
        part = jnp.dot(hidden, down_ref[:, span], preferred_element_type=jnp.float32)
        keep_ref[:, span] = part[:count]
        give_ref[:, span] = part[count:].astype(jnp.bfloat16)


def project(own, other, gate, up, down):
    count, features = own.shape
    units = gate.shape[0]
    whole = pl.BlockSpec(memory_space=pltpu.VMEM)
    return pl.pallas_call(
        expert_kernel,
        out_shape=(
            jax.ShapeDtypeStruct((count, features), jnp.float32),
            jax.ShapeDtypeStruct((count, features), jnp.bfloat16),
        ),
        in_specs=[whole] * 5,
        out_specs=(whole, whole),
        cost_estimate=pl.CostEstimate(
            flops=12 * count * features * units,
            bytes_accessed=6 * units * features + 10 * count * features,
            transcendentals=2 * count * units,
        ),
        compiler_params=pltpu.CompilerParams(vmem_limit_bytes=40 * 1024 * 1024),
        name="expert",
    )(own, other, gate, up, down)


def half(values):
    return values.astype(jnp.bfloat16)


def wide(values):
    return values.astype(jnp.float32)


def gathered_sums(arrived, gate, up, down):
    size = arrived.shape[0]
    length = lax.axis_size("z")
    outward = [(z * 2 + c, (z + 1 - 2 * c) % length * 2 + c) for z in range(length) for c in (0, 1)]
    inward = [(b, a) for a, b in outward]
    reach = length // 2
    pieces = [arrived]
    block = jnp.concatenate([arrived, lax.ppermute(arrived, "c", SWAP)])
    for step in range(1, reach + 1):
        if step == reach:
            block = block[:size]
        block = lax.ppermute(block, RING, outward)
        pieces.append(block)
    sums = []
    for piece in pieces:
        count = piece.shape[0]
        own = jnp.concatenate([piece, lax.ppermute(piece, "xl", SWAP)])
        keep, give = project(own, lax.ppermute(own, "c", SWAP), gate, up, down)
        total = keep + wide(lax.ppermute(give, "c", SWAP))
        crossed = lax.ppermute(half(total[count:]), "xl", SWAP)
        sums.append(total[:count] + wide(crossed))
    running = sums[reach]
    for step in range(reach - 1, 0, -1):
        came = wide(lax.ppermute(half(running), RING, inward))
        if step == reach - 1:
            running = jnp.concatenate([sums[step][:size] + came, sums[step][size:]])
        else:
            running = sums[step] + came
    came = lax.ppermute(half(running), RING, inward)
    swapped = lax.ppermute(came[size:], "c", SWAP)
    return half(sums[0] + wide(came[:size]) + wide(swapped))


def local(tokens, routes, route_weights, w_gate, w_up, w_down):
    groups = lax.axis_size("xh") * lax.axis_size("y")
    tok_count = tokens.shape[0]
    features = tokens.shape[1]
    capacity = 3 * tok_count // groups
    columns = groups * capacity
    gate, up, down = load(
        jnp.swapaxes(w_gate[0], 0, 1), jnp.swapaxes(w_up[0], 0, 1), w_down[0]
    )
    listed = routes.reshape(2 * tok_count)
    chosen = (listed[:, None] == jnp.arange(groups, dtype=jnp.int32)[None, :]).astype(jnp.int32)
    before = jnp.cumsum(chosen, axis=0) - chosen
    column = listed * capacity + jnp.sum(before * chosen, axis=1)
    placing = (column[:, None] == jnp.arange(columns, dtype=jnp.int32)[None, :]).astype(
        jnp.bfloat16
    )
    placing = placing.reshape(tok_count, 2, columns)
    sending = jnp.sum(placing, axis=1)
    outgoing = jnp.einsum("tw,td->wd", sending, tokens, preferred_element_type=jnp.float32).astype(
        jnp.bfloat16
    )
    arrived = lax.all_to_all(
        outgoing.reshape(groups, capacity, features), EXPERT, split_axis=0, concat_axis=0, tiled=True
    )
    results = gathered_sums(arrived.reshape(columns, features), gate, up, down)
    returned = lax.all_to_all(
        results.reshape(groups, capacity, features), EXPERT, split_axis=0, concat_axis=0, tiled=True
    ).reshape(columns, features)
    picked = jnp.einsum("tkw,wd->tkd", placing, returned, preferred_element_type=jnp.float32)
    combined = jnp.sum(route_weights[:, :, None] * picked, axis=1)
    return combined.astype(jnp.bfloat16)


def solution(mesh):
    fine = Mesh(mesh.devices.reshape(2, 4, 2, 8, 2), ALL)
    placed = (
        P(ALL, None),
        P(ALL, None),
        P(ALL, None),
        P(EXPERT, None, ("xl", "z", "c")),
        P(EXPERT, None, ("xl", "z", "c")),
        P(EXPERT, ("xl", "z", "c"), None),
    )
    return jax.shard_map(
        local, mesh=fine, in_specs=placed, out_specs=P(ALL, None), check_vma=False
    )
```

```python
import jax
import jax.numpy as jnp
from jax import lax
from jax.sharding import Mesh
from jax.sharding import PartitionSpec as P
from jax.experimental import pallas as pl
from jax.experimental.pallas import tpu as pltpu

EXPERT = ("xh", "y")
ALL = ("xh", "y", "xl", "z", "c")
RING = ("z", "c")
SWAP = [(0, 1), (1, 0)]
CUTS = 4


def expert_kernel(own_ref, other_ref, gate_ref, up_ref, down_ref, keep_ref, give_ref):
    count, features = own_ref.shape
    across = (((1,), (1,)), ((), ()))
    block = jnp.concatenate([own_ref[...], other_ref[...]], axis=0)
    gated = lax.dot_general(block, gate_ref[...], across, preferred_element_type=jnp.float32)
    upward = lax.dot_general(block, up_ref[...], across, preferred_element_type=jnp.float32)
    hidden = (gated / (1.0 + jnp.exp(-gated)) * upward).astype(jnp.bfloat16)
    depth = features // CUTS
    for cut in range(CUTS):
        span = pl.ds(cut * depth, depth)
        part = jnp.dot(hidden, down_ref[:, span], preferred_element_type=jnp.float32)
        keep_ref[:, span] = part[:count]
        give_ref[:, span] = part[count:].astype(jnp.bfloat16)


def project(own, other, gate, up, down):
    count, features = own.shape
    units = gate.shape[0]
    whole = pl.BlockSpec(memory_space=pltpu.VMEM)
    return pl.pallas_call(
        expert_kernel,
        out_shape=(
            jax.ShapeDtypeStruct((count, features), jnp.float32),
            jax.ShapeDtypeStruct((count, features), jnp.bfloat16),
        ),
        in_specs=[whole] * 5,
        out_specs=(whole, whole),
        cost_estimate=pl.CostEstimate(
            flops=12 * count * features * units,
            bytes_accessed=6 * units * features + 10 * count * features,
            transcendentals=2 * count * units,
        ),
        compiler_params=pltpu.CompilerParams(vmem_limit_bytes=40 * 1024 * 1024),
        name="expert",
    )(own, other, gate, up, down)


def half(values):
    return values.astype(jnp.bfloat16)


def wide(values):
    return values.astype(jnp.float32)


def gathered_sums(arrived, gate, up, down):
    size = arrived.shape[0]
    length = lax.axis_size("z")
    outward = [(z * 2 + c, (z + 1 - 2 * c) % length * 2 + c) for z in range(length) for c in (0, 1)]
    inward = [(b, a) for a, b in outward]
    reach = length // 2
    pieces = [arrived]
    block = jnp.concatenate([arrived, lax.ppermute(arrived, "c", SWAP)])
    for step in range(1, reach + 1):
        if step == reach:
            block = block[:size]
        block = lax.ppermute(block, RING, outward)
        pieces.append(block)
    sums = []
    for piece in pieces:
        count = piece.shape[0]
        own = jnp.concatenate([piece, lax.ppermute(piece, "xl", SWAP)])
        other = lax.ppermute(own, "c", SWAP)
        keep, give = project(own, other, gate, up, down)
        total = keep + wide(lax.ppermute(give, "c", SWAP))
        crossed = lax.ppermute(half(total[count:]), "xl", SWAP)
        sums.append(total[:count] + wide(crossed))
    running = sums[reach]
    for step in range(reach - 1, 0, -1):
        came = wide(lax.ppermute(half(running), RING, inward))
        if step == reach - 1:
            running = jnp.concatenate([sums[step][:size] + came, sums[step][size:]])
        else:
            running = sums[step] + came
    came = lax.ppermute(half(running), RING, inward)
    swapped = lax.ppermute(came[size:], "c", SWAP)
    return half(sums[0] + wide(came[:size]) + wide(swapped))


def local(tokens, routes, route_weights, w_gate, w_up, w_down):
    groups = lax.axis_size("xh") * lax.axis_size("y")
    tok_count = tokens.shape[0]
    features = tokens.shape[1]
    capacity = 3 * tok_count // groups
    columns = groups * capacity
    gate = jnp.swapaxes(w_gate[0], 0, 1)
    up = jnp.swapaxes(w_up[0], 0, 1)
    down = w_down[0]
    listed = routes.reshape(2 * tok_count)
    chosen = (listed[:, None] == jnp.arange(groups, dtype=jnp.int32)[None, :]).astype(jnp.int32)
    before = jnp.cumsum(chosen, axis=0) - chosen
    column = listed * capacity + jnp.sum(before * chosen, axis=1)
    placing = (column[:, None] == jnp.arange(columns, dtype=jnp.int32)[None, :]).astype(
        jnp.bfloat16
    )
    placing = placing.reshape(tok_count, 2, columns)
    sending = jnp.sum(placing, axis=1)
    outgoing = jnp.einsum("tw,td->wd", sending, tokens, preferred_element_type=jnp.float32).astype(
        jnp.bfloat16
    )
    arrived = lax.all_to_all(
        outgoing.reshape(groups, capacity, features), EXPERT, split_axis=0, concat_axis=0, tiled=True
    )
    results = gathered_sums(arrived.reshape(columns, features), gate, up, down)
    returned = lax.all_to_all(
        results.reshape(groups, capacity, features), EXPERT, split_axis=0, concat_axis=0, tiled=True
    ).reshape(columns, features)
    picked = jnp.einsum("tkw,wd->tkd", placing, returned, preferred_element_type=jnp.float32)
    combined = jnp.sum(route_weights[:, :, None] * picked, axis=1)
    return combined.astype(jnp.bfloat16)


def solution(mesh):
    fine = Mesh(mesh.devices.reshape(2, 4, 2, 8, 2), ALL)
    placed = (
        P(ALL, None),
        P(ALL, None),
        P(ALL, None),
        P(EXPERT, None, ("xl", "z", "c")),
        P(EXPERT, None, ("xl", "z", "c")),
        P(EXPERT, ("xl", "z", "c"), None),
    )
    return jax.shard_map(
        local, mesh=fine, in_specs=placed, out_specs=P(ALL, None), check_vma=False
    )
```

```python
import jax
import jax.numpy as jnp
from jax import lax
from jax.sharding import Mesh
from jax.sharding import PartitionSpec as P
from jax.experimental import pallas as pl
from jax.experimental.pallas import tpu as pltpu

EXPERT = ("xh", "y")
ALL = ("xh", "y", "xl", "z", "c")
RING = ("z", "c")
SWAP = [(0, 1), (1, 0)]
CUTS = 4


def load_kernel(gate_in, up_in, down_in, gate, up, down, sems):
    copies = []
    for which, (source, target) in enumerate(((gate_in, gate), (up_in, up), (down_in, down))):
        depth = source.shape[1] // CUTS
        for cut in range(CUTS):
            span = pl.ds(cut * depth, depth)
            copies.append(
                pltpu.make_async_copy(
                    source.at[:, span], target.at[:, span], sems.at[which * CUTS + cut]
                )
            )
    for copy in copies:
        copy.start()
    for copy in copies:
        copy.wait()


def load(*weights):
    whole = pl.BlockSpec(memory_space=pltpu.VMEM)
    outside = pl.BlockSpec(memory_space=pltpu.HBM)
    return pl.pallas_call(
        load_kernel,
        out_shape=[pltpu.VMEM(w.shape, w.dtype) for w in weights],
        in_specs=[outside] * 3,
        out_specs=[whole] * 3,
        scratch_shapes=[pltpu.SemaphoreType.DMA((3 * CUTS,))],
        compiler_params=pltpu.CompilerParams(vmem_limit_bytes=1024 * 1024),
        name="load",
    )(*[pltpu.with_memory_space_constraint(w, pltpu.HBM) for w in weights])


def expert_kernel(own_ref, other_ref, gate_ref, up_ref, down_ref, keep_ref, give_ref):
    count, features = own_ref.shape
    across = (((1,), (1,)), ((), ()))
    depth = features // CUTS
    gated = jnp.zeros((2 * count, gate_ref.shape[0]), jnp.float32)
    upward = jnp.zeros((2 * count, gate_ref.shape[0]), jnp.float32)
    for cut in range(CUTS):
        span = pl.ds(cut * depth, depth)
        block = jnp.concatenate([own_ref[:, span], other_ref[:, span]], axis=0)
        gated += lax.dot_general(
            block, gate_ref[:, span], across, preferred_element_type=jnp.float32
        )
        upward += lax.dot_general(block, up_ref[:, span], across, preferred_element_type=jnp.float32)
    hidden = (gated / (1.0 + jnp.exp(-gated)) * upward).astype(jnp.bfloat16)
    for cut in range(CUTS):
        span = pl.ds(cut * depth, depth)
        part = jnp.dot(hidden, down_ref[:, span], preferred_element_type=jnp.float32)
        keep_ref[:, span] = part[:count]
        give_ref[:, span] = part[count:].astype(jnp.bfloat16)


def project(own, other, gate, up, down):
    count, features = own.shape
    units = gate.shape[0]
    whole = pl.BlockSpec(memory_space=pltpu.VMEM)
    return pl.pallas_call(
        expert_kernel,
        out_shape=(
            jax.ShapeDtypeStruct((count, features), jnp.float32),
            jax.ShapeDtypeStruct((count, features), jnp.bfloat16),
        ),
        in_specs=[whole] * 5,
        out_specs=(whole, whole),
        cost_estimate=pl.CostEstimate(
            flops=12 * count * features * units,
            bytes_accessed=6 * units * features + 10 * count * features,
            transcendentals=2 * count * units,
        ),
        compiler_params=pltpu.CompilerParams(vmem_limit_bytes=24 * 1024 * 1024),
        name="expert",
    )(own, other, gate, up, down)


def half(values):
    return values.astype(jnp.bfloat16)


def wide(values):
    return values.astype(jnp.float32)


def gathered_sums(arrived, gate, up, down):
    size = arrived.shape[0]
    length = lax.axis_size("z")
    outward = [(z * 2 + c, (z + 1 - 2 * c) % length * 2 + c) for z in range(length) for c in (0, 1)]
    inward = [(b, a) for a, b in outward]
    reach = length // 2
    pieces = [arrived]
    block = jnp.concatenate([arrived, lax.ppermute(arrived, "c", SWAP)])
    for step in range(1, reach + 1):
        if step == reach:
            block = block[:size]
        block = lax.ppermute(block, RING, outward)
        pieces.append(block)
    sums = []
    for piece in pieces:
        count = piece.shape[0]
        own = jnp.concatenate([piece, lax.ppermute(piece, "xl", SWAP)])
        other = lax.ppermute(own, "c", SWAP)
        keep, give = project(own, other, gate, up, down)
        total = keep + wide(lax.ppermute(give, "c", SWAP))
        crossed = lax.ppermute(half(total[count:]), "xl", SWAP)
        sums.append(total[:count] + wide(crossed))
    running = sums[reach]
    for step in range(reach - 1, 0, -1):
        came = wide(lax.ppermute(half(running), RING, inward))
        if step == reach - 1:
            running = jnp.concatenate([sums[step][:size] + came, sums[step][size:]])
        else:
            running = sums[step] + came
    came = lax.ppermute(half(running), RING, inward)
    swapped = lax.ppermute(came[size:], "c", SWAP)
    return half(sums[0] + wide(came[:size]) + wide(swapped))


def local(tokens, routes, route_weights, w_gate, w_up, w_down):
    groups = lax.axis_size("xh") * lax.axis_size("y")
    tok_count = tokens.shape[0]
    features = tokens.shape[1]
    capacity = 3 * tok_count // groups
    columns = groups * capacity
    gate, up, down = load(
        jnp.swapaxes(w_gate[0], 0, 1), jnp.swapaxes(w_up[0], 0, 1), w_down[0]
    )
    listed = routes.reshape(2 * tok_count)
    chosen = (listed[:, None] == jnp.arange(groups, dtype=jnp.int32)[None, :]).astype(jnp.int32)
    before = jnp.cumsum(chosen, axis=0) - chosen
    column = listed * capacity + jnp.sum(before * chosen, axis=1)
    placing = (column[:, None] == jnp.arange(columns, dtype=jnp.int32)[None, :]).astype(
        jnp.bfloat16
    )
    placing = placing.reshape(tok_count, 2, columns)
    sending = jnp.sum(placing, axis=1)
    outgoing = jnp.einsum("tw,td->wd", sending, tokens, preferred_element_type=jnp.float32).astype(
        jnp.bfloat16
    )
    arrived = lax.all_to_all(
        outgoing.reshape(groups, capacity, features), EXPERT, split_axis=0, concat_axis=0, tiled=True
    )
    results = gathered_sums(arrived.reshape(columns, features), gate, up, down)
    returned = lax.all_to_all(
        results.reshape(groups, capacity, features), EXPERT, split_axis=0, concat_axis=0, tiled=True
    ).reshape(columns, features)
    picked = jnp.einsum("tkw,wd->tkd", placing, returned, preferred_element_type=jnp.float32)
    combined = jnp.sum(route_weights[:, :, None] * picked, axis=1)
    return combined.astype(jnp.bfloat16)


def solution(mesh):
    fine = Mesh(mesh.devices.reshape(2, 4, 2, 8, 2), ALL)
    placed = (
        P(ALL, None),
        P(ALL, None),
        P(ALL, None),
        P(EXPERT, None, ("xl", "z", "c")),
        P(EXPERT, None, ("xl", "z", "c")),
        P(EXPERT, ("xl", "z", "c"), None),
    )
    return jax.shard_map(
        local, mesh=fine, in_specs=placed, out_specs=P(ALL, None), check_vma=False
    )
```

```python
import jax
import jax.numpy as jnp
from jax import lax
from jax.sharding import Mesh
from jax.sharding import PartitionSpec as P
from jax.experimental import pallas as pl
from jax.experimental.pallas import tpu as pltpu

EXPERT = ("xh", "y")
ALL = ("xh", "y", "xl", "z", "c")
RING = ("z", "c")
SWAP = [(0, 1), (1, 0)]
CUTS = 4


def load_kernel(gate_in, up_in, down_in, gate, up, down, sems):
    copies = []
    for which, (source, target) in enumerate(((gate_in, gate), (up_in, up), (down_in, down))):
        depth = source.shape[1] // CUTS
        for cut in range(CUTS):
            span = pl.ds(cut * depth, depth)
            copies.append(
                pltpu.make_async_copy(
                    source.at[:, span], target.at[:, span], sems.at[which * CUTS + cut]
                )
            )
    for copy in copies:
        copy.start()
    for copy in copies:
        copy.wait()


def load(*weights):
    whole = pl.BlockSpec(memory_space=pltpu.VMEM)
    outside = pl.BlockSpec(memory_space=pltpu.HBM)
    return pl.pallas_call(
        load_kernel,
        out_shape=[pltpu.VMEM(w.shape, w.dtype) for w in weights],
        in_specs=[outside] * 3,
        out_specs=[whole] * 3,
        scratch_shapes=[pltpu.SemaphoreType.DMA((3 * CUTS,))],
        compiler_params=pltpu.CompilerParams(vmem_limit_bytes=1024 * 1024),
        name="load",
    )(*[pltpu.with_memory_space_constraint(w, pltpu.HBM) for w in weights])


def expert_kernel(own_ref, other_ref, gate_ref, up_ref, down_ref, keep_ref, give_ref):
    count, features = own_ref.shape
    across = (((1,), (1,)), ((), ()))
    depth = features // CUTS
    gated = jnp.zeros((2 * count, gate_ref.shape[0]), jnp.float32)
    upward = jnp.zeros((2 * count, gate_ref.shape[0]), jnp.float32)
    for cut in range(CUTS):
        span = pl.ds(cut * depth, depth)
        block = jnp.concatenate([own_ref[:, span], other_ref[:, span]], axis=0)
        gated += lax.dot_general(
            block, gate_ref[:, span], across, preferred_element_type=jnp.float32
        )
        upward += lax.dot_general(block, up_ref[:, span], across, preferred_element_type=jnp.float32)
    hidden = (gated / (1.0 + jnp.exp(-gated)) * upward).astype(jnp.bfloat16)
    for cut in range(CUTS):
        span = pl.ds(cut * depth, depth)
        part = jnp.dot(hidden, down_ref[:, span], preferred_element_type=jnp.float32)
        keep_ref[:, span] = part[:count]
        give_ref[:, span] = part[count:].astype(jnp.bfloat16)


def project(own, other, gate, up, down):
    count, features = own.shape
    units = gate.shape[0]
    whole = pl.BlockSpec(memory_space=pltpu.VMEM)
    return pl.pallas_call(
        expert_kernel,
        out_shape=(
            jax.ShapeDtypeStruct((count, features), jnp.float32),
            jax.ShapeDtypeStruct((count, features), jnp.bfloat16),
        ),
        in_specs=[whole] * 5,
        out_specs=(whole, whole),
        cost_estimate=pl.CostEstimate(
            flops=12 * count * features * units,
            bytes_accessed=6 * units * features + 10 * count * features,
            transcendentals=2 * count * units,
        ),
        compiler_params=pltpu.CompilerParams(vmem_limit_bytes=24 * 1024 * 1024),
        name="expert",
    )(own, other, gate, up, down)


def half(values):
    return values.astype(jnp.bfloat16)


def wide(values):
    return values.astype(jnp.float32)


def gathered_sums(arrived, gate, up, down):
    size = arrived.shape[0]
    length = lax.axis_size("z")
    outward = [(z * 2 + c, (z + 1 - 2 * c) % length * 2 + c) for z in range(length) for c in (0, 1)]
    inward = [(b, a) for a, b in outward]
    reach = length // 2
    pieces = [arrived]
    block = jnp.concatenate([arrived, lax.ppermute(arrived, "c", SWAP)])
    for _ in range(1, reach):
        block = lax.ppermute(block, RING, outward)
        pieces.append(block)
    opposite = [(z, (z + reach) % length) for z in range(length)]
    pieces.append(lax.ppermute(arrived, "z", opposite))
    sums = []
    for piece in pieces:
        count = piece.shape[0]
        side = lax.ppermute(piece, "xl", SWAP)
        own = jnp.concatenate([piece, side])
        other = lax.ppermute(own, "c", SWAP)
        keep, give = project(own, other, gate, up, down)
        total = keep + wide(lax.ppermute(give, "c", SWAP))
        crossed = lax.ppermute(half(total[count:]), "xl", SWAP)
        sums.append(total[:count] + wide(crossed))
    running = sums[reach]
    for step in range(reach - 1, 0, -1):
        came = wide(lax.ppermute(half(running), RING, inward))
        if step == reach - 1:
            running = jnp.concatenate([sums[step][:size] + came, sums[step][size:]])
        else:
            running = sums[step] + came
    came = lax.ppermute(half(running), RING, inward)
    swapped = lax.ppermute(came[size:], "c", SWAP)
    return half(sums[0] + wide(came[:size]) + wide(swapped))


def local(tokens, routes, route_weights, w_gate, w_up, w_down):
    groups = lax.axis_size("xh") * lax.axis_size("y")
    tok_count = tokens.shape[0]
    features = tokens.shape[1]
    capacity = 3 * tok_count // groups
    columns = groups * capacity
    gate, up, down = load(
        jnp.swapaxes(w_gate[0], 0, 1), jnp.swapaxes(w_up[0], 0, 1), w_down[0]
    )
    listed = routes.reshape(2 * tok_count)
    chosen = (listed[:, None] == jnp.arange(groups, dtype=jnp.int32)[None, :]).astype(jnp.int32)
    before = jnp.cumsum(chosen, axis=0) - chosen
    column = listed * capacity + jnp.sum(before * chosen, axis=1)
    placing = (column[:, None] == jnp.arange(columns, dtype=jnp.int32)[None, :]).astype(
        jnp.bfloat16
    )
    placing = placing.reshape(tok_count, 2, columns)
    sending = jnp.sum(placing, axis=1)
    outgoing = jnp.einsum("tw,td->wd", sending, tokens, preferred_element_type=jnp.float32).astype(
        jnp.bfloat16
    )
    arrived = lax.all_to_all(
        outgoing.reshape(groups, capacity, features), EXPERT, split_axis=0, concat_axis=0, tiled=True
    )
    results = gathered_sums(arrived.reshape(columns, features), gate, up, down)
    returned = lax.all_to_all(
        results.reshape(groups, capacity, features), EXPERT, split_axis=0, concat_axis=0, tiled=True
    ).reshape(columns, features)
    picked = jnp.einsum("tkw,wd->tkd", placing, returned, preferred_element_type=jnp.float32)
    combined = jnp.sum(route_weights[:, :, None] * picked, axis=1)
    return combined.astype(jnp.bfloat16)


def solution(mesh):
    fine = Mesh(mesh.devices.reshape(2, 4, 2, 8, 2), ALL)
    placed = (
        P(ALL, None),
        P(ALL, None),
        P(ALL, None),
        P(EXPERT, None, ("xl", "z", "c")),
        P(EXPERT, None, ("xl", "z", "c")),
        P(EXPERT, ("xl", "z", "c"), None),
    )
    return jax.shard_map(
        local, mesh=fine, in_specs=placed, out_specs=P(ALL, None), check_vma=False
    )
```

```python
import jax
import jax.numpy as jnp
from jax import lax
from jax.sharding import Mesh
from jax.sharding import PartitionSpec as P
from jax.experimental import pallas as pl
from jax.experimental.pallas import tpu as pltpu

EXPERT = ("xh", "y")
ALL = ("xh", "y", "xl", "z", "c")
RING = ("z", "c")
SWAP = [(0, 1), (1, 0)]
CUTS = 4


def load_kernel(gate_in, up_in, down_in, gate, up, down, sems):
    copies = []
    for which, (source, target) in enumerate(((gate_in, gate), (up_in, up), (down_in, down))):
        depth = source.shape[1] // CUTS
        for cut in range(CUTS):
            span = pl.ds(cut * depth, depth)
            copies.append(
                pltpu.make_async_copy(
                    source.at[:, span], target.at[:, span], sems.at[which * CUTS + cut]
                )
            )
    for copy in copies:
        copy.start()
    for copy in copies:
        copy.wait()


def load(*weights):
    whole = pl.BlockSpec(memory_space=pltpu.VMEM)
    outside = pl.BlockSpec(memory_space=pltpu.HBM)
    return pl.pallas_call(
        load_kernel,
        out_shape=[pltpu.VMEM(w.shape, w.dtype) for w in weights],
        in_specs=[outside] * 3,
        out_specs=[whole] * 3,
        scratch_shapes=[pltpu.SemaphoreType.DMA((3 * CUTS,))],
        compiler_params=pltpu.CompilerParams(vmem_limit_bytes=1024 * 1024),
        name="load",
    )(*[pltpu.with_memory_space_constraint(w, pltpu.HBM) for w in weights])


def expert_kernel(own_ref, other_ref, gate_ref, up_ref, down_ref, keep_ref, give_ref):
    count, features = own_ref.shape
    across = (((1,), (1,)), ((), ()))
    depth = features // CUTS
    gated = jnp.zeros((2 * count, gate_ref.shape[0]), jnp.float32)
    upward = jnp.zeros((2 * count, gate_ref.shape[0]), jnp.float32)
    for cut in range(CUTS):
        span = pl.ds(cut * depth, depth)
        block = jnp.concatenate([own_ref[:, span], other_ref[:, span]], axis=0)
        gated += lax.dot_general(
            block, gate_ref[:, span], across, preferred_element_type=jnp.float32
        )
        upward += lax.dot_general(block, up_ref[:, span], across, preferred_element_type=jnp.float32)
    hidden = (gated / (1.0 + jnp.exp(-gated)) * upward).astype(jnp.bfloat16)
    for cut in range(CUTS):
        span = pl.ds(cut * depth, depth)
        part = jnp.dot(hidden, down_ref[:, span], preferred_element_type=jnp.float32)
        keep_ref[:, span] = part[:count]
        give_ref[:, span] = part[count:].astype(jnp.bfloat16)


def project(own, other, gate, up, down):
    count, features = own.shape
    units = gate.shape[0]
    whole = pl.BlockSpec(memory_space=pltpu.VMEM)
    return pl.pallas_call(
        expert_kernel,
        out_shape=(
            jax.ShapeDtypeStruct((count, features), jnp.float32),
            jax.ShapeDtypeStruct((count, features), jnp.bfloat16),
        ),
        in_specs=[whole] * 5,
        out_specs=(whole, whole),
        cost_estimate=pl.CostEstimate(
            flops=12 * count * features * units,
            bytes_accessed=6 * units * features + 10 * count * features,
            transcendentals=2 * count * units,
        ),
        compiler_params=pltpu.CompilerParams(vmem_limit_bytes=24 * 1024 * 1024),
        name="expert",
    )(own, other, gate, up, down)


def half(values):
    return values.astype(jnp.bfloat16)


def wide(values):
    return values.astype(jnp.float32)


def gathered_sums(arrived, gate, up, down):
    size = arrived.shape[0]
    length = lax.axis_size("z")
    outward = [(z * 2 + c, (z + 1 - 2 * c) % length * 2 + c) for z in range(length) for c in (0, 1)]
    inward = [(b, a) for a, b in outward]
    reach = length // 2
    pieces = [arrived]
    block = jnp.concatenate([arrived, lax.ppermute(arrived, "c", SWAP)])
    for step in range(1, reach + 1):
        if step == reach:
            block = block[:size]
        block = lax.ppermute(block, RING, outward)
        pieces.append(block)
    sums = []
    for piece in pieces:
        count = piece.shape[0]
        own = jnp.concatenate([piece, lax.ppermute(piece, "xl", SWAP)])
        other = lax.ppermute(own, "c", SWAP)
        keep, give = project(own, other, gate, up, down)
        taken = lax.ppermute(give, "c", SWAP)
        crossing = half(keep[count:] + wide(taken[count:]))
        crossed = lax.ppermute(crossing, "xl", SWAP)
        sums.append(keep[:count] + wide(taken[:count]) + wide(crossed))
    running = sums[reach]
    for step in range(reach - 1, 0, -1):
        came = wide(lax.ppermute(half(running), RING, inward))
        if step == reach - 1:
            running = jnp.concatenate([sums[step][:size] + came, sums[step][size:]])
        else:
            running = sums[step] + came
    came = lax.ppermute(half(running), RING, inward)
    swapped = lax.ppermute(came[size:], "c", SWAP)
    return half(sums[0] + wide(came[:size]) + wide(swapped))


def local(tokens, routes, route_weights, w_gate, w_up, w_down):
    groups = lax.axis_size("xh") * lax.axis_size("y")
    tok_count = tokens.shape[0]
    features = tokens.shape[1]
    capacity = 3 * tok_count // groups
    columns = groups * capacity
    gate, up, down = load(
        jnp.swapaxes(w_gate[0], 0, 1), jnp.swapaxes(w_up[0], 0, 1), w_down[0]
    )
    listed = routes.reshape(2 * tok_count)
    chosen = (listed[:, None] == jnp.arange(groups, dtype=jnp.int32)[None, :]).astype(jnp.int32)
    before = jnp.cumsum(chosen, axis=0) - chosen
    column = listed * capacity + jnp.sum(before * chosen, axis=1)
    placing = (column[:, None] == jnp.arange(columns, dtype=jnp.int32)[None, :]).astype(
        jnp.bfloat16
    )
    placing = placing.reshape(tok_count, 2, columns)
    sending = jnp.sum(placing, axis=1)
    outgoing = jnp.einsum("tw,td->wd", sending, tokens, preferred_element_type=jnp.float32).astype(
        jnp.bfloat16
    )
    arrived = lax.all_to_all(
        outgoing.reshape(groups, capacity, features), EXPERT, split_axis=0, concat_axis=0, tiled=True
    )
    results = gathered_sums(arrived.reshape(columns, features), gate, up, down)
    returned = lax.all_to_all(
        results.reshape(groups, capacity, features), EXPERT, split_axis=0, concat_axis=0, tiled=True
    ).reshape(columns, features)
    picked = jnp.einsum("tkw,wd->tkd", placing, returned, preferred_element_type=jnp.float32)
    combined = jnp.sum(route_weights[:, :, None] * picked, axis=1)
    return combined.astype(jnp.bfloat16)


def solution(mesh):
    fine = Mesh(mesh.devices.reshape(2, 4, 2, 8, 2), ALL)
    placed = (
        P(ALL, None),
        P(ALL, None),
        P(ALL, None),
        P(EXPERT, None, ("xl", "z", "c")),
        P(EXPERT, None, ("xl", "z", "c")),
        P(EXPERT, ("xl", "z", "c"), None),
    )
    return jax.shard_map(
        local, mesh=fine, in_specs=placed, out_specs=P(ALL, None), check_vma=False
    )
```
